32 devices in a mesh: fiber: 8 (over z, x), seg: 4 (over y, core).
Axes of the slice: x: 2, y: 2, z: 4, core: 2. Of those that a mesh axis runs over, the one named last changes fastest.
Arguments:
- raw_strain: bfloat16 [64, 1024, 2048], P('seg', 'fiber'), may hold values from -6 to 6
- fir_taps: float32 [31], replicated, may hold values from -1 to 1
- good_mask: int32 [64, 1024], P('seg', 'fiber'), may hold values from 0 to 1, as said below
Outputs:
- stacked_spectra: float32 [144, 1024, 2, 128], P('seg', 'fiber')
The draws below stay inside these ranges and needn't reach their ends.
Inputs may be any that keep to these rules, and one draw needn't show every extreme that they name: `good_mask`: 0 or 1; some channels are 0 in every segment.
All inputs are finite; a program needn't handle non-finite values.
Results may differ from the reference program's by a relative error of at most 0.005.
Values may be sent and summed in bfloat16 or wider, within the bound.
A program may use at most 192 MiB of HBM per device.

```python
import math
import jax
import jax.numpy as jnp
from jax import lax

SAMPLES = 2048
NF = 144
LOW = 16
HALF = 15
TAPS = 31
SMOOTH = 4
LAGS = 128
CH_DEV = 128
NCH = 1024
SEGS = 64


def draw_good_mask(key, part):
    key_dead = jax.random.fold_in(key, 11)
    key_drop = jax.random.fold_in(key, 12)
    alive = jax.random.randint(key_dead, (1, NCH), 0, 16) != 0
    kept = jax.random.randint(key_drop, (SEGS, NCH), 0, 5) != 0
    return (alive & kept).astype(jnp.int32)


def block_levels(key, shape, pieces, least, largest):
    level, own = 1.0, jax.random.fold_in(key, 6)
    for axis_at, parts in pieces:
        draws = jnp.exp(jax.random.uniform(jax.random.fold_in(own, axis_at), (parts,), jnp.float32, least / len(pieces), largest / len(pieces)))
        level = level * jnp.repeat(draws, shape[axis_at] // parts).reshape([-1 if axis == axis_at else 1 for axis in range(len(shape))])
    return level


def gaussian(rng, shape, scale, limit, split=(), held_as=jnp.bfloat16):
    loudness = block_levels(rng, shape, split, -0.22, 0.18) if split else 1.0
    values = jax.random.normal(rng, shape, jnp.float32) * scale * loudness
    return jnp.minimum(jnp.maximum(values, -limit), limit).astype(held_as)


def setup_inputs(seed: int = 0) -> dict:
    seeds = jax.random.split(jax.random.key(seed), 4)
    return {
        "raw_strain": gaussian(seeds[0], (SEGS, NCH, SAMPLES), 1.0, 6.0, ((0, 4), (1, 8))),
        "fir_taps": jnp.clip(jax.random.uniform(seeds[1], (TAPS,), jnp.float32, -1.0, 1.0), -1.0, 1.0),
        "good_mask": draw_good_mask(jax.random.fold_in(seeds[3], 71), 0),
    }


epsilon = 1e-06
water_share = 0.1

def dft_basis(samples):
    times = jnp.arange(samples, dtype=jnp.int32)
    bins = jnp.arange(NF, dtype=jnp.int32) + LOW
    phase_index = times[:, None] * bins[None, :] % samples
    angles = phase_index.astype(jnp.float32) * (2.0 * math.pi / samples)
    return jnp.stack([jnp.cos(angles), -jnp.sin(angles)], axis=2).astype(jnp.bfloat16)

def lag_band(gram):
    lead = gram.shape[:-2]
    rows = gram.shape[-2]
    cols = gram.shape[-1]
    flat = gram.reshape(lead + (rows * cols,))
    padding = [(0, 0)] * len(lead) + [(0, rows)]
    flat = jnp.pad(flat, padding)
    skewed = flat.reshape(lead + (rows, cols + 1))
    return skewed[..., 1:1 + LAGS]

def whiten(filtered, good_mask):
    powers = filtered[:, :, 0] * filtered[:, :, 0] + filtered[:, :, 1] * filtered[:, :, 1]
    bin_count = powers.shape[1]
    padded = jnp.pad(powers, ((0, 0), (SMOOTH, SMOOTH), (0, 0)))
    smooth = padded[:, 0:bin_count]
    for offset in range(1, 2 * SMOOTH + 1):
        smooth = smooth + padded[:, offset:offset + bin_count]
    smooth = smooth / (2 * SMOOTH + 1)
    water_level = lax.optimization_barrier(jnp.mean(powers, axis=1, keepdims=True))
    divisor = jnp.sqrt(smooth + water_share * water_level + epsilon)
    scaled = good_mask.astype(jnp.float32)[:, None, :] / divisor
    return (filtered * scaled[:, :, None, :]).astype(jnp.bfloat16)

def cross_band(left_block, extended):
    rotated = jnp.stack([extended[:, :, 1], -extended[:, :, 0]], axis=2)
    gram_real = jnp.einsum('sfrc,sfrd->fcd', left_block, extended, precision=lax.Precision.HIGHEST)
    gram_imag = jnp.einsum('sfrc,sfrd->fcd', left_block, rotated, precision=lax.Precision.HIGHEST)
    return jnp.stack([lag_band(gram_real), lag_band(gram_imag)], axis=2)

def reference(raw_strain, fir_taps, good_mask):
    basis = dft_basis(SAMPLES).astype(jnp.float32)

    def one_segment(inputs):
        segment, segment_mask = inputs
        spectra = jnp.einsum('ct,tfr->frc', segment.astype(jnp.float32), basis, precision=lax.Precision.HIGHEST)
        padded = jnp.pad(spectra, ((0, 0), (0, 0), (HALF, HALF)))
        filtered = fir_taps[0] * padded[:, :, 0:NCH]
        for tap_index in range(1, 2 * HALF + 1):
            filtered = filtered + fir_taps[tap_index] * padded[:, :, tap_index:tap_index + NCH]
        return whiten(filtered[None], segment_mask[None])[0]
    whitened = lax.map(one_segment, (raw_strain, good_mask))
    padded_white = jnp.pad(whitened, ((0, 0), (0, 0), (0, 0), (0, CH_DEV)))
    mask_float = good_mask.astype(jnp.float32)
    padded_mask = jnp.pad(mask_float, ((0, 0), (0, CH_DEV)))

    def one_block(block_index):
        first = (block_index * CH_DEV).astype(jnp.int32)
        left_block = lax.dynamic_slice_in_dim(whitened, first, CH_DEV, 3).astype(jnp.float32)
        extended = lax.dynamic_slice_in_dim(padded_white, first, 2 * CH_DEV, 3).astype(jnp.float32)
        sums = cross_band(left_block, extended)
        mask_left = lax.dynamic_slice_in_dim(mask_float, first, CH_DEV, 1)
        mask_wide = lax.dynamic_slice_in_dim(padded_mask, first, 2 * CH_DEV, 1)
        counts = lag_band(jnp.einsum('sc,sd->cd', mask_left, mask_wide, precision=lax.Precision.HIGHEST))
        return sums / jnp.maximum(counts, 1.0)[None, :, None, :]
    blocks = lax.map(one_block, jnp.arange(NCH // CH_DEV, dtype=jnp.int32))
    return jnp.transpose(blocks, (1, 0, 2, 3, 4)).reshape(NF, NCH, 2, LAGS)
```

```python
import functools
import math

import jax
import jax.numpy as jnp
import numpy as np
from jax import lax
from jax.experimental import pallas as pl
from jax.experimental.pallas import tpu as pltpu
from jax.sharding import PartitionSpec as P

NF = 144
LOW = 16
SMOOTH = 4
LAGS = 128
EDGE = 16

epsilon = 1e-06
water_share = 0.1
MESH = pl.DeviceIdType.MESH


def row_bins(shares):
    per = NF // shares
    return np.concatenate([np.tile(np.arange(k * per, (k + 1) * per), 2) for k in range(shares)])


def row_parts(shares):
    per = NF // shares
    return np.tile(np.repeat(np.arange(2), per), shares)


def dft_rows(samples, shares):
    bins, parts = row_bins(shares), row_parts(shares)
    index = ((bins[:, None] + LOW) * np.arange(samples)[None, :]) % samples
    angles = index.astype(np.float64) * (2.0 * math.pi / samples)
    return np.where(parts[:, None] == 0, np.cos(angles), -np.sin(angles)).astype(jnp.bfloat16)


def smooth_rows(shares):
    bins = row_bins(shares)
    return (np.abs(bins[:, None] - bins[None, :]) <= SMOOTH).astype(jnp.bfloat16)


def two_terms(x):
    hi = x.astype(jnp.bfloat16)
    return hi, (x - hi.astype(jnp.float32)).astype(jnp.bfloat16)


def mm(a, b):
    return jnp.dot(a, b, preferred_element_type=jnp.float32)


def mm_t(a, b):
    return lax.dot_general(a, b, (((1,), (1,)), ((), ())), preferred_element_type=jnp.float32)


def spectra_kernel(
    fibers, shares, taps_ref, raw_ref, mask_ref, basis_ref, smooth_ref,
    own_ref, next_ref,
    raw_v, edge_v, spec_v, out_l, out_r, in_l, in_r, band_v, mask_v, white_v, send_v,
    raw_sem, edge_sem, halo_send, halo_recv, send_sem, recv_sem, local_sem,
):
    fib = lax.axis_index("fiber")
    seg = lax.axis_index("seg")
    segs, channels, _ = raw_ref.shape
    rows = basis_ref.shape[0]
    per = rows // shares
    taps = taps_ref.shape[0]
    half = (taps - 1) // 2
    has_prev = fib > 0
    has_next = fib < fibers - 1

    edge_copies = [
        pltpu.make_async_copy(raw_ref.at[:, pl.ds(start, EDGE), :], edge_v.at[i], edge_sem.at[i])
        for i, start in enumerate((0, channels - EDGE))
    ]
    for copy in edge_copies:
        copy.start()
    pairs = segs // 2
    raw_copies = [
        pltpu.make_async_copy(raw_ref.at[pl.ds(2 * p, 2)], raw_v.at[p], raw_sem.at[p])
        for p in range(pairs)
    ]
    for copy in raw_copies:
        copy.start()

    barrier = pltpu.get_barrier_semaphore()
    for d in range(1, shares):
        pl.semaphore_signal(
            barrier, inc=1, device_id=(fib, lax.rem(seg + d, shares)), device_id_type=MESH
        )
    @pl.when(has_prev)
    def _():
        for k in range(shares):
            pl.semaphore_signal(barrier, inc=1, device_id=(fib - 1, k), device_id_type=MESH)
    @pl.when(has_next)
    def _():
        for k in range(shares):
            pl.semaphore_signal(barrier, inc=1, device_id=(fib + 1, k), device_id_type=MESH)

    row = lax.broadcasted_iota(jnp.int32, (2 * channels, channels), 0)
    col = lax.broadcasted_iota(jnp.int32, (2 * channels, channels), 1)
    left = row - channels - EDGE
    right = row - EDGE
    place = jnp.where(row < channels, row, jnp.where(left < 0, left, right))
    place = jnp.where(row < channels + 2 * EDGE, place, 8 * channels)
    tap = place - col + half
    band = jnp.zeros((2 * channels, channels), jnp.float32)
    for j in range(taps):
        band = jnp.where(tap == j, taps_ref[j], band)
    band_hi, band_lo = two_terms(band)
    band_v[:, :channels] = band_hi
    band_v[:, channels:] = band_lo
    mask_v[...] = mask_ref[...].astype(jnp.float32)
    for k in range(shares):
        send_v[k, per] = mask_ref[...].astype(jnp.float32).astype(jnp.bfloat16)

    @pl.when(jnp.logical_not(has_prev))
    def _():
        in_l[...] = jnp.zeros_like(in_l)
    @pl.when(jnp.logical_not(has_next))
    def _():
        in_r[...] = jnp.zeros_like(in_r)
        next_ref[...] = jnp.zeros_like(next_ref)

    edge_copies[0].wait()
    out_l[...] = mm_t(basis_ref[...], edge_v[0].reshape(segs * EDGE, -1))
    edge_copies[1].wait()
    out_r[...] = mm_t(basis_ref[...], edge_v[1].reshape(segs * EDGE, -1))

    sides = (fib + fibers - 1) // fibers + (2 * fibers - 2 - fib) // fibers
    pl.semaphore_wait(barrier, shares - 1 + shares * sides)

    to_prev = pltpu.make_async_remote_copy(
        src_ref=out_l, dst_ref=in_r, send_sem=halo_send.at[0], recv_sem=halo_recv.at[0],
        device_id=(jnp.maximum(fib - 1, 0), seg), device_id_type=MESH,
    )
    to_next = pltpu.make_async_remote_copy(
        src_ref=out_r, dst_ref=in_l, send_sem=halo_send.at[1], recv_sem=halo_recv.at[1],
        device_id=(jnp.minimum(fib + 1, fibers - 1), seg), device_id_type=MESH,
    )
    @pl.when(has_prev)
    def _():
        to_prev.start()
    @pl.when(has_next)
    def _():
        to_next.start()

    for p in range(pairs):
        raw_copies[p].wait()
        spec_v[p] = mm_t(basis_ref[...], raw_v[p].reshape(2 * channels, -1))

    @pl.when(has_prev)
    def _():
        to_next.wait_recv()
    @pl.when(has_next)
    def _():
        to_prev.wait_recv()

    per_tile = channels // EDGE
    lane = lax.broadcasted_iota(jnp.int32, (rows, channels), 1)

    def whiten_pair(p, carry):
        group = (2 * p) // per_tile
        base = pl.multiple_of(group * channels, channels)
        lefts = in_l[:, pl.ds(base, channels)]
        rights = in_r[:, pl.ds(base, channels)]
        parts = []
        for h in range(2):
            slot = lax.rem(2 * p + h, per_tile)
            l_roll = lax.rem(channels - slot * EDGE, channels)
            r_roll = lax.rem(channels + EDGE - slot * EDGE, channels)
            edges = jnp.where(
                lane < EDGE, pltpu.roll(lefts, l_roll, 1), pltpu.roll(rights, r_roll, 1)
            )
            both = jnp.concatenate([spec_v[p, :, h * channels : (h + 1) * channels], edges], axis=1)
            hi, lo = two_terms(both)
            wide = mm(hi, band_v[...])
            parts.append(
                wide[:, :channels] + wide[:, channels:] + mm(lo, band_v[:, :channels])
            )
        filtered = jnp.concatenate(parts, axis=1)
        power = filtered * filtered
        hi, lo = two_terms(power)
        smooth = mm(smooth_ref[...], hi) + mm(smooth_ref[...], lo)
        total = jnp.sum(power, axis=0, keepdims=True)
        level = smooth * (1.0 / (2 * SMOOTH + 1)) + (total * (water_share / NF) + epsilon)
        good = jnp.concatenate([mask_v[pl.ds(2 * p, 1), :], mask_v[pl.ds(2 * p + 1, 1), :]], axis=1)
        white = filtered * (lax.rsqrt(level) * good)
        white_v[pl.ds(2 * p, rows, segs), :] = white[:, :channels]
        white_v[pl.ds(2 * p + 1, rows, segs), :] = white[:, channels:]
        return carry

    lax.fori_loop(0, pairs, whiten_pair, 0)

    prev = jnp.maximum(fib - 1, 0)
    later = []
    own = []
    for k in range(shares):
        send_v[k, :per] = (
            white_v[k * per * segs : (k + 1) * per * segs, :]
            .reshape(per, segs, channels)
            .astype(jnp.bfloat16)
        )
        later.append(
            pltpu.make_async_remote_copy(
                src_ref=send_v.at[k], dst_ref=next_ref.at[seg],
                send_sem=send_sem.at[k], recv_sem=recv_sem.at[seg],
                device_id=(prev, k), device_id_type=MESH,
            )
        )
        @pl.when(has_prev)
        def _():
            later[k].start()
    for d in range(1, shares):
        other = lax.rem(seg + d, shares)
        own.append(
            pltpu.make_async_remote_copy(
                src_ref=send_v.at[other], dst_ref=own_ref.at[seg],
                send_sem=send_sem.at[shares + d], recv_sem=recv_sem.at[shares + seg],
                device_id=(fib, other), device_id_type=MESH,
            )
        )
        own[-1].start()
    mine = pltpu.make_async_copy(send_v.at[seg], own_ref.at[seg], local_sem.at[0])
    mine.start()
    mine.wait()
    for d in range(1, shares):
        source = lax.rem(seg + d, shares)
        pltpu.make_async_remote_copy(
            src_ref=send_v.at[source], dst_ref=own_ref.at[source],
            send_sem=send_sem.at[shares + d], recv_sem=recv_sem.at[shares + source],
            device_id=(fib, source), device_id_type=MESH,
        ).wait_recv()
    @pl.when(has_next)
    def _():
        for k in range(shares):
            pltpu.make_async_remote_copy(
                src_ref=send_v.at[k], dst_ref=next_ref.at[k],
                send_sem=send_sem.at[k], recv_sem=recv_sem.at[k],
                device_id=(prev, k), device_id_type=MESH,
            ).wait_recv()
    for copy in own:
        copy.wait_send()
    @pl.when(has_prev)
    def _():
        for copy in later:
            copy.wait_send()
        to_prev.wait_send()
    @pl.when(has_next)
    def _():
        to_next.wait_send()


def cross_kernel(step_bins, own_ref, next_ref, out_ref, scale_v):
    i = pl.program_id(0)
    shares, rows, segs, channels = own_ref.shape
    bins = (rows - 1) // 2
    depth = shares * segs
    row = lax.broadcasted_iota(jnp.int32, (channels, channels), 0)
    col = lax.broadcasted_iota(jnp.int32, (channels, channels), 1)

    lags = (col + row + 1) % channels

    def taken(ref, q):
        return ref[:, q].reshape(depth, channels)

    def lagged(near, far):
        chosen = jnp.where(col > row, near, far)
        return jnp.take_along_axis(chosen, lags, axis=1)

    def grams(a, b):
        return lax.dot_general(a, b, (((0,), (0,)), ((), ())), preferred_element_type=jnp.float32)

    @pl.when(i == 0)
    def _():
        here = taken(own_ref, rows - 1)
        counts = lagged(grams(here, here), grams(here, taken(next_ref, rows - 1)))
        scale_v[...] = 1.0 / jnp.maximum(counts, 1.0)

    scale = scale_v[...]
    for b in range(step_bins):
        f = i * step_bins + b
        own_re, own_im = taken(own_ref, f), taken(own_ref, bins + f)
        next_re, next_im = taken(next_ref, f), taken(next_ref, bins + f)
        left = jnp.concatenate([own_re, own_im], axis=0)
        top = jnp.concatenate([own_re, next_re, own_im, next_im], axis=1)
        low = jnp.concatenate([own_im, next_im, -own_re, -next_re], axis=1)
        gram = grams(left, jnp.concatenate([top, low], axis=0))
        cells = [gram[:, n * channels : (n + 1) * channels] for n in range(4)]
        out_ref[b, pl.ds(0, channels, 2), :] = lagged(cells[0], cells[1]) * scale
        out_ref[b, pl.ds(1, channels, 2), :] = lagged(cells[2], cells[3]) * scale


def on_device(raw_strain, fir_taps, good_mask):
    segs, channels, samples = raw_strain.shape
    fibers, shares = lax.axis_size("fiber"), lax.axis_size("seg")
    rows = 2 * NF
    per = rows // shares
    block = jax.ShapeDtypeStruct((shares, per + 1, segs, channels), jnp.bfloat16)
    vmem = pl.BlockSpec(memory_space=pltpu.VMEM)
    edges = (rows, segs * EDGE)
    own, later = pl.pallas_call(
        functools.partial(spectra_kernel, fibers, shares),
        out_shape=(block, block),
        in_specs=[
            pl.BlockSpec(memory_space=pltpu.SMEM),
            pl.BlockSpec(memory_space=pltpu.HBM),
            vmem, vmem, vmem,
        ],
        out_specs=(vmem, vmem),
        scratch_shapes=[
            pltpu.VMEM((segs // 2, 2, channels, samples), jnp.bfloat16),
            pltpu.VMEM((2, segs, EDGE, samples), jnp.bfloat16),
            pltpu.VMEM((segs // 2, rows, 2 * channels), jnp.float32),
            pltpu.VMEM(edges, jnp.float32),
            pltpu.VMEM(edges, jnp.float32),
            pltpu.VMEM(edges, jnp.float32),
            pltpu.VMEM(edges, jnp.float32),
            pltpu.VMEM((2 * channels, 2 * channels), jnp.bfloat16),
            pltpu.VMEM((segs, channels), jnp.float32),
            pltpu.VMEM((rows * segs, channels), jnp.float32),
            pltpu.VMEM(block.shape, jnp.bfloat16),
            pltpu.SemaphoreType.DMA((segs // 2,)),
            pltpu.SemaphoreType.DMA((2,)),
            pltpu.SemaphoreType.DMA((2,)),
            pltpu.SemaphoreType.DMA((2,)),
            pltpu.SemaphoreType.DMA((2 * shares,)),
            pltpu.SemaphoreType.DMA((2 * shares,)),
            pltpu.SemaphoreType.DMA((1,)),
        ],
        compiler_params=pltpu.CompilerParams(
            collective_id=0, has_side_effects=True, vmem_limit_bytes=40 * 2**20
        ),
        name="spectra",
    )(fir_taps, raw_strain, good_mask, dft_rows(samples, shares), smooth_rows(shares))

    bins = NF // shares
    step_bins = next(n for n in (4, 3, 2, 1) if bins % n == 0)
    out = pl.pallas_call(
        functools.partial(cross_kernel, step_bins),
        grid=(bins // step_bins,),
        out_shape=jax.ShapeDtypeStruct((bins, 2 * channels, LAGS), jnp.float32),
        in_specs=[vmem, vmem],
        out_specs=pl.BlockSpec((step_bins, 2 * channels, LAGS), lambda i: (i, 0, 0)),
        scratch_shapes=[pltpu.VMEM((channels, LAGS), jnp.float32)],
        compiler_params=pltpu.CompilerParams(vmem_limit_bytes=40 * 2**20),
        name="cross",
    )(own, later)
    return out.reshape(bins, channels, 2, LAGS)


def solution(mesh):
    return jax.shard_map(
        on_device,
        mesh=mesh,
        in_specs=(P("seg", "fiber", None), P(), P("seg", "fiber")),
        out_specs=P("seg", "fiber", None, None),
        check_vma=False,
    )
```

```python
import functools
import math

import jax
import jax.numpy as jnp
import numpy as np
from jax import lax
from jax.experimental import pallas as pl
from jax.experimental.pallas import tpu as pltpu
from jax.sharding import PartitionSpec as P

NF = 144
LOW = 16
SMOOTH = 4
LAGS = 128
EDGE = 16

epsilon = 1e-06
water_share = 0.1
MESH = pl.DeviceIdType.MESH
VMEM_LIMIT = 40 * 2**20


def row_bins(shares):
    per = NF // shares
    return np.concatenate([np.tile(np.arange(k * per, (k + 1) * per), 2) for k in range(shares)])


def row_parts(shares):
    per = NF // shares
    return np.tile(np.repeat(np.arange(2), per), shares)


def dft_rows(samples, shares):
    bins, parts = row_bins(shares), row_parts(shares)
    index = ((bins[:, None] + LOW) * np.arange(samples)[None, :]) % samples
    angles = index.astype(np.float64) * (2.0 * math.pi / samples)
    return np.where(parts[:, None] == 0, np.cos(angles), -np.sin(angles)).astype(jnp.bfloat16)


def smooth_rows(shares):
    bins = row_bins(shares)
    return (np.abs(bins[:, None] - bins[None, :]) <= SMOOTH).astype(jnp.bfloat16)


def two_terms(x):
    hi = x.astype(jnp.bfloat16)
    return hi, (x - hi.astype(jnp.float32)).astype(jnp.bfloat16)


def mm(a, b):
    return jnp.dot(a, b, preferred_element_type=jnp.float32)


def mm_t(a, b):
    return lax.dot_general(a, b, (((1,), (1,)), ((), ())), preferred_element_type=jnp.float32)


def partner(seg, m):
    bit = 1
    while bit <= m:
        if m & bit:
            seg = seg + bit - 2 * bit * (seg // bit % 2)
        bit *= 2
    return seg


def spectra_kernel(
    fibers, shares, taps_ref, raw_ref, mask_ref, basis_hbm, smooth_hbm,
    own_ref, next_ref,
    raw_v, edge_v, basis_ref, smooth_ref, flag_v, spec_v, out_l, out_r, in_l, in_r, band_v, mask_v,
    white_v, send_v,
    raw_sem, edge_sem, halo_send, halo_recv, own_send, own_recv, next_send, next_recv, local_sem,
):
    fib = lax.axis_index("fiber")
    seg = lax.axis_index("seg")
    segs, channels, _ = raw_ref.shape
    rows = basis_ref.shape[0]
    per = rows // shares
    taps = taps_ref.shape[0]
    half = (taps - 1) // 2
    has_prev = fib > 0
    has_next = fib < fibers - 1
    prev = jnp.maximum(fib - 1, 0)
    following = jnp.minimum(fib + 1, fibers - 1)
    size = channels // EDGE
    chunks = segs // size
    pairs = segs // 2
    chunk_pairs = size // 2

    basis_copy = pltpu.make_async_copy(basis_hbm, basis_ref, edge_sem.at[2])
    basis_copy.start()
    edge_copies = [
        pltpu.make_async_copy(raw_ref.at[:, pl.ds(start, EDGE), :], edge_v.at[i], edge_sem.at[i])
        for i, start in enumerate((0, channels - EDGE))
    ]
    for copy in edge_copies:
        copy.start()
    mask_copy = pltpu.make_async_copy(mask_ref, flag_v, edge_sem.at[4])
    mask_copy.start()
    raw_copies = [
        pltpu.make_async_copy(raw_ref.at[pl.ds(2 * p, 2)], raw_v.at[p], raw_sem.at[p])
        for p in range(pairs)
    ]
    for copy in raw_copies:
        copy.start()
    smooth_copy = pltpu.make_async_copy(smooth_hbm, smooth_ref, edge_sem.at[3])
    smooth_copy.start()

    barrier = pltpu.get_barrier_semaphore()
    for m in range(1, shares):
        pl.semaphore_signal(
            barrier, inc=1, device_id=(fib, partner(seg, m)), device_id_type=MESH
        )
    @pl.when(has_prev)
    def _():
        pl.semaphore_signal(barrier, inc=1, device_id=(fib - 1, seg), device_id_type=MESH)
    @pl.when(has_next)
    def _():
        pl.semaphore_signal(barrier, inc=1, device_id=(fib + 1, seg), device_id_type=MESH)

    row = lax.broadcasted_iota(jnp.int32, (2 * channels, channels), 0)
    col = lax.broadcasted_iota(jnp.int32, (2 * channels, channels), 1)
    left = row - channels - EDGE
    right = row - EDGE
    place = jnp.where(row < channels, row, jnp.where(left < 0, left, right))
    place = jnp.where(row < channels + 2 * EDGE, place, 8 * channels)
    tap = place - col + half
    band = jnp.zeros((2 * channels, channels), jnp.float32)
    for j in range(taps):
        band = jnp.where(tap == j, taps_ref[j], band)
    band_hi, band_lo = two_terms(band)
    band_v[:, :channels] = band_hi
    band_v[:, channels:] = band_lo

    @pl.when(jnp.logical_not(has_prev))
    def _():
        in_l[...] = jnp.zeros_like(in_l)
    @pl.when(jnp.logical_not(has_next))
    def _():
        in_r[...] = jnp.zeros_like(in_r)
        next_ref[...] = jnp.zeros_like(next_ref)

    basis_copy.wait()
    for edge, out in ((0, out_l), (1, out_r)):
        edge_copies[edge].wait()
        ends = mm_t(basis_ref[...], edge_v[edge].reshape(segs * EDGE, -1)).astype(jnp.bfloat16)
        for c in range(chunks):
            out[c] = ends[:, c * channels : (c + 1) * channels]

    sides = (fib + fibers - 1) // fibers + (2 * fibers - 2 - fib) // fibers
    pl.semaphore_wait(barrier, shares - 1 + sides)

    to_prev = [
        pltpu.make_async_remote_copy(
            src_ref=out_l.at[c], dst_ref=in_r.at[c],
            send_sem=halo_send.at[0, c], recv_sem=halo_recv.at[0, c],
            device_id=(prev, seg), device_id_type=MESH,
        )
        for c in range(chunks)
    ]
    to_next = [
        pltpu.make_async_remote_copy(
            src_ref=out_r.at[c], dst_ref=in_l.at[c],
            send_sem=halo_send.at[1, c], recv_sem=halo_recv.at[1, c],
            device_id=(following, seg), device_id_type=MESH,
        )
        for c in range(chunks)
    ]
    for c in range(chunks):
        @pl.when(has_prev)
        def _():
            to_prev[c].start()
        @pl.when(has_next)
        def _():
            to_next[c].start()

    mask_copy.wait()
    mask_v[...] = flag_v[...].astype(jnp.float32)
    for c in range(chunks):
        flags = mask_v[c * size : (c + 1) * size, :].astype(jnp.bfloat16)
        for k in range(shares):
            send_v[k, c, per] = flags

    lane = lax.broadcasted_iota(jnp.int32, (rows, channels), 1)

    def transform(c):
        for p in range(c * chunk_pairs, (c + 1) * chunk_pairs):
            raw_copies[p].wait()
            spec_v[p] = mm_t(basis_ref[...], raw_v[p].reshape(2 * channels, -1))

    def whiten(c):
        def whiten_pair(i, carry):
            p = c * chunk_pairs + i
            lefts = in_l[c].astype(jnp.float32)
            rights = in_r[c].astype(jnp.float32)
            parts = []
            for h in range(2):
                slot = 2 * i + h
                l_roll = lax.rem(channels - slot * EDGE, channels)
                r_roll = lax.rem(channels + EDGE - slot * EDGE, channels)
                edges = jnp.where(
                    lane < EDGE, pltpu.roll(lefts, l_roll, 1), pltpu.roll(rights, r_roll, 1)
                )
                hi, lo = two_terms(spec_v[p, :, h * channels : (h + 1) * channels])
                wide = mm(jnp.concatenate([hi, edges.astype(jnp.bfloat16)], axis=1), band_v[...])
                parts.append(
                    wide[:, :channels] + wide[:, channels:] + mm(lo, band_v[:channels, :channels])
                )
            filtered = jnp.concatenate(parts, axis=1)
            power = filtered * filtered
            hi, lo = two_terms(power)
            smooth = mm(smooth_ref[...], hi) + mm(smooth_ref[...], lo)
            total = jnp.sum(power, axis=0, keepdims=True)
            level = smooth * (1.0 / (2 * SMOOTH + 1)) + (total * (water_share / NF) + epsilon)
            good = jnp.concatenate(
                [mask_v[pl.ds(2 * p, 1), :], mask_v[pl.ds(2 * p + 1, 1), :]], axis=1
            )
            white = filtered * (lax.rsqrt(level) * good)
            white_v[pl.ds(2 * i, rows, size), :] = white[:, :channels]
            white_v[pl.ds(2 * i + 1, rows, size), :] = white[:, channels:]
            return carry

        lax.fori_loop(0, chunk_pairs, whiten_pair, 0)
        for k in range(shares):
            send_v[k, c, :per] = (
                white_v[k * per * size : (k + 1) * per * size, :]
                .reshape(per, size, channels)
                .astype(jnp.bfloat16)
            )

    def to_own(c, m):
        other = partner(seg, m)
        return pltpu.make_async_remote_copy(
            src_ref=send_v.at[other, c], dst_ref=own_ref.at[seg, c],
            send_sem=own_send.at[c, m], recv_sem=own_recv.at[c, m],
            device_id=(fib, other), device_id_type=MESH,
        )

    def from_own(c, m):
        other = partner(seg, m)
        return pltpu.make_async_remote_copy(
            src_ref=send_v.at[other, c], dst_ref=own_ref.at[other, c],
            send_sem=own_send.at[c, m], recv_sem=own_recv.at[c, m],
            device_id=(fib, other), device_id_type=MESH,
        )

    def hand_on(c, m):
        source = partner(seg, m)
        block = send_v if m == 0 else own_ref
        return pltpu.make_async_remote_copy(
            src_ref=block.at[source, c], dst_ref=next_ref.at[source, c],
            send_sem=next_send.at[c, m], recv_sem=next_recv.at[c, m],
            device_id=(prev, seg), device_id_type=MESH,
        )

    def kept(c):
        return pltpu.make_async_copy(send_v.at[seg, c], own_ref.at[seg, c], local_sem.at[c])

    def give(c):
        @pl.when(has_prev)
        def _():
            hand_on(c, 0).start()
        for m in range(1, shares):
            to_own(c, m).start()
        kept(c).start()

    def relay(c, m):
        from_own(c, m).wait_recv()
        @pl.when(has_prev)
        def _():
            hand_on(c, m).start()

    smooth_copy.wait()
    waiting = []
    for c in range(chunks):
        transform(c)
        if waiting:
            relay(*waiting.pop(0))
        @pl.when(has_prev)
        def _():
            to_next[c].wait_recv()
        @pl.when(has_next)
        def _():
            to_prev[c].wait_recv()
        whiten(c)
        give(c)
        waiting += [(c, m) for m in range(1, shares)]
    for item in waiting:
        relay(*item)
    for c in range(chunks):
        kept(c).wait()
        for m in range(1, shares):
            to_own(c, m).wait_send()
    @pl.when(has_prev)
    def _():
        for c in range(chunks):
            to_prev[c].wait_send()
            for m in range(shares):
                hand_on(c, m).wait_send()
    @pl.when(has_next)
    def _():
        for c in range(chunks):
            to_next[c].wait_send()
            for m in range(shares):
                hand_on(c, m).wait_recv()


def cross_kernel(step_bins, own_ref, next_ref, out_ref, scale_v):
    i = pl.program_id(0)
    shares, chunks, rows, size, channels = own_ref.shape
    bins = (rows - 1) // 2
    depth = shares * chunks * size
    row = lax.broadcasted_iota(jnp.int32, (channels, channels), 0)
    col = lax.broadcasted_iota(jnp.int32, (channels, channels), 1)

    lags = (col + row + 1) % channels

    def taken(ref, q):
        return ref[:, :, q].reshape(depth, channels)

    def lagged(near, far):
        chosen = jnp.where(col > row, near, far)
        return jnp.take_along_axis(chosen, lags, axis=1)

    def grams(a, b):
        return lax.dot_general(a, b, (((0,), (0,)), ((), ())), preferred_element_type=jnp.float32)

    @pl.when(i == 0)
    def _():
        here = taken(own_ref, rows - 1)
        counts = lagged(grams(here, here), grams(here, taken(next_ref, rows - 1)))
        scale_v[...] = 1.0 / jnp.maximum(counts, 1.0)

    scale = scale_v[...]
    for b in range(step_bins):
        f = i * step_bins + b
        own_re, own_im = taken(own_ref, f), taken(own_ref, bins + f)
        next_re, next_im = taken(next_ref, f), taken(next_ref, bins + f)
        left = jnp.concatenate([own_re, own_im], axis=0)
        top = jnp.concatenate([own_re, next_re, own_im, next_im], axis=1)
        low = jnp.concatenate([own_im, next_im, -own_re, -next_re], axis=1)
        gram = grams(left, jnp.concatenate([top, low], axis=0))
        cells = [gram[:, n * channels : (n + 1) * channels] for n in range(4)]
        out_ref[b, pl.ds(0, channels, 2), :] = lagged(cells[0], cells[1]) * scale
        out_ref[b, pl.ds(1, channels, 2), :] = lagged(cells[2], cells[3]) * scale


def on_device(raw_strain, fir_taps, good_mask):
    segs, channels, samples = raw_strain.shape
    fibers, shares = lax.axis_size("fiber"), lax.axis_size("seg")
    rows = 2 * NF
    per = rows // shares
    size = channels // EDGE
    chunks = segs // size
    block = jax.ShapeDtypeStruct((shares, chunks, per + 1, size, channels), jnp.bfloat16)
    vmem = pl.BlockSpec(memory_space=pltpu.VMEM)
    hbm = pl.BlockSpec(memory_space=pltpu.HBM)
    edges = pltpu.VMEM((chunks, rows, size * EDGE), jnp.bfloat16)
    basis, smooth = dft_rows(samples, shares), smooth_rows(shares)
    dma = pltpu.SemaphoreType.DMA
    own, later = pl.pallas_call(
        functools.partial(spectra_kernel, fibers, shares),
        out_shape=(block, block),
        in_specs=[pl.BlockSpec(memory_space=pltpu.SMEM), hbm, hbm, hbm, hbm],
        out_specs=(vmem, vmem),
        scratch_shapes=[
            pltpu.VMEM((segs // 2, 2, channels, samples), jnp.bfloat16),
            pltpu.VMEM((2, segs, EDGE, samples), jnp.bfloat16),
            pltpu.VMEM(basis.shape, jnp.bfloat16),
            pltpu.VMEM(smooth.shape, jnp.bfloat16),
            pltpu.VMEM((segs, channels), jnp.int32),
            pltpu.VMEM((segs // 2, rows, 2 * channels), jnp.float32),
            edges, edges, edges, edges,
            pltpu.VMEM((2 * channels, 2 * channels), jnp.bfloat16),
            pltpu.VMEM((segs, channels), jnp.float32),
            pltpu.VMEM((rows * size, channels), jnp.float32),
            pltpu.VMEM(block.shape, jnp.bfloat16),
            dma((segs // 2,)),
            dma((5,)),
            dma((2, chunks)),
            dma((2, chunks)),
            dma((chunks, shares)),
            dma((chunks, shares)),
            dma((chunks, shares)),
            dma((chunks, shares)),
            dma((chunks,)),
        ],
        compiler_params=pltpu.CompilerParams(
            collective_id=0, has_side_effects=True, vmem_limit_bytes=VMEM_LIMIT
        ),
        name="spectra",
    )(
        fir_taps,
        *(
            pltpu.with_memory_space_constraint(x, pltpu.HBM)
            for x in (raw_strain, good_mask, jnp.asarray(basis), jnp.asarray(smooth))
        ),
    )

    bins = NF // shares
    step_bins = next(n for n in (4, 3, 2, 1) if bins % n == 0)
    out = pl.pallas_call(
        functools.partial(cross_kernel, step_bins),
        grid=(bins // step_bins,),
        out_shape=jax.ShapeDtypeStruct((bins, 2 * channels, LAGS), jnp.float32),
        in_specs=[vmem, vmem],
        out_specs=pl.BlockSpec((step_bins, 2 * channels, LAGS), lambda i: (i, 0, 0)),
        scratch_shapes=[pltpu.VMEM((channels, LAGS), jnp.float32)],
        compiler_params=pltpu.CompilerParams(vmem_limit_bytes=40 * 2**20),
        name="cross",
    )(own, later)
    return out.reshape(bins, channels, 2, LAGS)


def solution(mesh):
    return jax.shard_map(
        on_device,
        mesh=mesh,
        in_specs=(P("seg", "fiber", None), P(), P("seg", "fiber")),
        out_specs=P("seg", "fiber", None, None),
        check_vma=False,
    )
```

```python
import functools
import math

import jax
import jax.numpy as jnp
import numpy as np
from jax import lax
from jax.experimental import pallas as pl
from jax.experimental.pallas import tpu as pltpu
from jax.sharding import PartitionSpec as P

NF = 144
LOW = 16
SMOOTH = 4
LAGS = 128
EDGE = 16

epsilon = 1e-06
water_share = 0.1
MESH = pl.DeviceIdType.MESH
VMEM_LIMIT = 40 * 2**20


def row_bins(shares):
    per = NF // shares
    return np.concatenate([np.tile(np.arange(k * per, (k + 1) * per), 2) for k in range(shares)])


def row_parts(shares):
    per = NF // shares
    return np.tile(np.repeat(np.arange(2), per), shares)


def dft_rows(samples, shares):
    bins, parts = row_bins(shares), row_parts(shares)
    index = ((bins[:, None] + LOW) * np.arange(samples)[None, :]) % samples
    angles = index.astype(np.float64) * (2.0 * math.pi / samples)
    return np.where(parts[:, None] == 0, np.cos(angles), -np.sin(angles)).astype(jnp.bfloat16)


def smooth_rows(shares):
    bins = row_bins(shares)
    return (np.abs(bins[:, None] - bins[None, :]) <= SMOOTH).astype(jnp.bfloat16)


def two_terms(x):
    hi = x.astype(jnp.bfloat16)
    return hi, (x - hi.astype(jnp.float32)).astype(jnp.bfloat16)


def mm(a, b):
    return jnp.dot(a, b, preferred_element_type=jnp.float32)


def mm_t(a, b):
    return lax.dot_general(a, b, (((1,), (1,)), ((), ())), preferred_element_type=jnp.float32)


def turned(x, shift):
    return pltpu.roll(x, shift, 1) if shift else x


def partner(seg, m):
    bit = 1
    while bit <= m:
        if m & bit:
            seg = seg + bit - 2 * bit * (seg // bit % 2)
        bit *= 2
    return seg


def spectra_kernel(
    fibers, shares, taps_ref, raw_ref, mask_ref, basis_hbm, smooth_hbm,
    own_ref, next_ref,
    raw_v, edge_v, basis_ref, smooth_ref, flag_v, spec_v, out_l, out_r, in_l, in_r, band_v, mask_v,
    white_v, send_v,
    raw_sem, edge_sem, misc_sem, halo_send, halo_recv, own_send, own_recv, next_send, next_recv, local_sem,
):
    fib = lax.axis_index("fiber")
    seg = lax.axis_index("seg")
    segs, channels, _ = raw_ref.shape
    rows = basis_ref.shape[0]
    per = rows // shares
    taps = taps_ref.shape[0]
    half = (taps - 1) // 2
    has_prev = fib > 0
    has_next = fib < fibers - 1
    prev = jnp.maximum(fib - 1, 0)
    following = jnp.minimum(fib + 1, fibers - 1)
    size = channels // EDGE
    chunks = segs // size
    pairs = segs // 2
    chunk_pairs = size // 2

    basis_copy = pltpu.make_async_copy(basis_hbm, basis_ref, misc_sem.at[0])
    basis_copy.start()
    edge_copies = [
        [
            pltpu.make_async_copy(
                raw_ref.at[pl.ds(c * size, size), pl.ds(start, EDGE), :],
                edge_v.at[c, i], edge_sem.at[2 * c + i],
            )
            for i, start in enumerate((0, channels - EDGE))
        ]
        for c in range(chunks)
    ]
    for copy in edge_copies[0]:
        copy.start()
    mask_copy = pltpu.make_async_copy(mask_ref, flag_v, misc_sem.at[2])
    mask_copy.start()
    raw_copies = [
        pltpu.make_async_copy(raw_ref.at[pl.ds(2 * p, 2)], raw_v.at[p], raw_sem.at[p])
        for p in range(pairs)
    ]
    for p, copy in enumerate(raw_copies):
        copy.start()
        if (p + 1) % chunk_pairs == 0 and (p + 1) // chunk_pairs < chunks:
            for edge in edge_copies[(p + 1) // chunk_pairs]:
                edge.start()
    smooth_copy = pltpu.make_async_copy(smooth_hbm, smooth_ref, misc_sem.at[1])
    smooth_copy.start()

    barrier = pltpu.get_barrier_semaphore()
    for m in range(1, shares):
        pl.semaphore_signal(
            barrier, inc=1, device_id=(fib, partner(seg, m)), device_id_type=MESH
        )
    @pl.when(has_prev)
    def _():
        pl.semaphore_signal(barrier, inc=1, device_id=(fib - 1, seg), device_id_type=MESH)
    @pl.when(has_next)
    def _():
        pl.semaphore_signal(barrier, inc=1, device_id=(fib + 1, seg), device_id_type=MESH)

    row = lax.broadcasted_iota(jnp.int32, (2 * channels, channels), 0)
    col = lax.broadcasted_iota(jnp.int32, (2 * channels, channels), 1)
    left = row - channels - EDGE
    right = row - EDGE
    place = jnp.where(row < channels, row, jnp.where(left < 0, left, right))
    place = jnp.where(row < channels + 2 * EDGE, place, 8 * channels)
    tap = place - col + half
    band = jnp.zeros((2 * channels, channels), jnp.float32)
    for j in range(taps):
        band = jnp.where(tap == j, taps_ref[j], band)
    band_hi, band_lo = two_terms(band)
    band_v[:, :channels] = band_hi
    band_v[:, channels:] = band_lo

    @pl.when(jnp.logical_not(has_prev))
    def _():
        in_l[...] = jnp.zeros_like(in_l)
    @pl.when(jnp.logical_not(has_next))
    def _():
        in_r[...] = jnp.zeros_like(in_r)
        next_ref[...] = jnp.zeros_like(next_ref)

    def transform_edges(c):
        for copy in edge_copies[c]:
            copy.wait()
        ends = mm_t(basis_ref[...], edge_v[c].reshape(2 * channels, -1)).astype(jnp.bfloat16)
        out_l[c] = ends[:, :channels]
        out_r[c] = ends[:, channels:]

    basis_copy.wait()
    transform_edges(0)
    sides = (fib + fibers - 1) // fibers + (2 * fibers - 2 - fib) // fibers
    pl.semaphore_wait(barrier, shares - 1 + sides)

    to_prev = [
        pltpu.make_async_remote_copy(
            src_ref=out_l.at[c], dst_ref=in_r.at[c],
            send_sem=halo_send.at[0, c], recv_sem=halo_recv.at[0, c],
            device_id=(prev, seg), device_id_type=MESH,
        )
        for c in range(chunks)
    ]
    to_next = [
        pltpu.make_async_remote_copy(
            src_ref=out_r.at[c], dst_ref=in_l.at[c],
            send_sem=halo_send.at[1, c], recv_sem=halo_recv.at[1, c],
            device_id=(following, seg), device_id_type=MESH,
        )
        for c in range(chunks)
    ]
    def send_edges(c):
        @pl.when(has_prev)
        def _():
            to_prev[c].start()
        @pl.when(has_next)
        def _():
            to_next[c].start()

    send_edges(0)
    mask_copy.wait()
    mask_v[...] = flag_v[...].astype(jnp.float32)
    for c in range(chunks):
        flags = mask_v[c * size : (c + 1) * size, :].astype(jnp.bfloat16)
        for k in range(shares):
            send_v[k, c, per] = flags

    lane = lax.broadcasted_iota(jnp.int32, (rows, channels), 1)

    def transform(c):
        for p in range(c * chunk_pairs, (c + 1) * chunk_pairs):
            raw_copies[p].wait()
            spec_v[p] = mm_t(basis_ref[...], raw_v[p].reshape(2 * channels, -1))

    def whiten(c):
        def whiten_pair(i, carry):
            p = c * chunk_pairs + i
            lefts = in_l[c].astype(jnp.float32)
            rights = in_r[c].astype(jnp.float32)
            parts = []
            for h in range(2):
                slot = 2 * i + h
                l_roll = (channels - slot * EDGE) % channels
                r_roll = (channels + EDGE - slot * EDGE) % channels
                edges = jnp.where(lane < EDGE, turned(lefts, l_roll), turned(rights, r_roll))
                hi, lo = two_terms(spec_v[p, :, h * channels : (h + 1) * channels])
                wide = mm(jnp.concatenate([hi, edges.astype(jnp.bfloat16)], axis=1), band_v[...])
                parts.append(
                    wide[:, :channels] + wide[:, channels:] + mm(lo, band_v[:channels, :channels])
                )
            filtered = jnp.concatenate(parts, axis=1)
            power = filtered * filtered
            smooth = mm(smooth_ref[...], power.astype(jnp.bfloat16))
            total = jnp.sum(power, axis=0, keepdims=True)
            level = smooth * (1.0 / (2 * SMOOTH + 1)) + (total * (water_share / NF) + epsilon)
            good = jnp.concatenate(
                [mask_v[pl.ds(2 * p, 1), :], mask_v[pl.ds(2 * p + 1, 1), :]], axis=1
            )
            white = filtered * (lax.rsqrt(level) * good)
            white_v[pl.ds(2 * i, rows, size), :] = white[:, :channels]
            white_v[pl.ds(2 * i + 1, rows, size), :] = white[:, channels:]
            return carry

        for i in range(chunk_pairs):
            whiten_pair(i, 0)
        for k in range(shares):
            send_v[k, c, :per] = (
                white_v[k * per * size : (k + 1) * per * size, :]
                .reshape(per, size, channels)
                .astype(jnp.bfloat16)
            )

    def to_own(c, m):
        other = partner(seg, m)
        return pltpu.make_async_remote_copy(
            src_ref=send_v.at[other, c], dst_ref=own_ref.at[seg, c],
            send_sem=own_send.at[c, m], recv_sem=own_recv.at[c, m],
            device_id=(fib, other), device_id_type=MESH,
        )

    def from_own(c, m):
        other = partner(seg, m)
        return pltpu.make_async_remote_copy(
            src_ref=send_v.at[other, c], dst_ref=own_ref.at[other, c],
            send_sem=own_send.at[c, m], recv_sem=own_recv.at[c, m],
            device_id=(fib, other), device_id_type=MESH,
        )

    def hand_on(c, m):
        source = partner(seg, m)
        block = send_v if m == 0 else own_ref
        return pltpu.make_async_remote_copy(
            src_ref=block.at[source, c], dst_ref=next_ref.at[source, c],
            send_sem=next_send.at[c, m], recv_sem=next_recv.at[c, m],
            device_id=(prev, seg), device_id_type=MESH,
        )

    def kept(c):
        return pltpu.make_async_copy(send_v.at[seg, c], own_ref.at[seg, c], local_sem.at[c])

    def give(c):
        @pl.when(has_prev)
        def _():
            hand_on(c, 0).start()
        for m in range(1, shares):
            to_own(c, m).start()
        kept(c).start()

    def relay(c, m):
        from_own(c, m).wait_recv()
        @pl.when(has_prev)
        def _():
            hand_on(c, m).start()

    smooth_copy.wait()
    waiting = []
    for c in range(chunks):
        transform(c)
        if c + 1 < chunks:
            transform_edges(c + 1)
            send_edges(c + 1)
        if waiting:
            relay(*waiting.pop(0))
        @pl.when(has_prev)
        def _():
            to_next[c].wait_recv()
        @pl.when(has_next)
        def _():
            to_prev[c].wait_recv()
        whiten(c)
        give(c)
        waiting += [(c, m) for m in range(1, shares)]
    for item in waiting:
        relay(*item)
    for c in range(chunks):
        kept(c).wait()
        for m in range(1, shares):
            to_own(c, m).wait_send()
    @pl.when(has_prev)
    def _():
        for c in range(chunks):
            to_prev[c].wait_send()
            for m in range(shares):
                hand_on(c, m).wait_send()
    @pl.when(has_next)
    def _():
        for c in range(chunks):
            to_next[c].wait_send()
            for m in range(shares):
                hand_on(c, m).wait_recv()


def cross_kernel(step_bins, own_ref, next_ref, out_ref, scale_v):
    i = pl.program_id(0)
    shares, chunks, rows, size, channels = own_ref.shape
    bins = (rows - 1) // 2
    depth = shares * chunks * size
    row = lax.broadcasted_iota(jnp.int32, (channels, channels), 0)
    col = lax.broadcasted_iota(jnp.int32, (channels, channels), 1)

    lags = (col + row + 1) % channels

    def taken(ref, q):
        return ref[:, :, q].reshape(depth, channels)

    def lagged(near, far):
        chosen = jnp.where(col > row, near, far)
        return jnp.take_along_axis(chosen, lags, axis=1)

    def grams(a, b):
        return lax.dot_general(a, b, (((0,), (0,)), ((), ())), preferred_element_type=jnp.float32)

    @pl.when(i == 0)
    def _():
        here = taken(own_ref, rows - 1)
        counts = lagged(grams(here, here), grams(here, taken(next_ref, rows - 1)))
        scale_v[...] = 1.0 / jnp.maximum(counts, 1.0)

    scale = scale_v[...]
    for b in range(step_bins):
        f = i * step_bins + b
        own_re, own_im = taken(own_ref, f), taken(own_ref, bins + f)
        next_re, next_im = taken(next_ref, f), taken(next_ref, bins + f)
        left = jnp.concatenate([own_re, own_im], axis=0)
        top = jnp.concatenate([own_re, next_re, own_im, next_im], axis=1)
        low = jnp.concatenate([own_im, next_im, -own_re, -next_re], axis=1)
        gram = grams(left, jnp.concatenate([top, low], axis=0))
        cells = [gram[:, n * channels : (n + 1) * channels] for n in range(4)]
        out_ref[b, pl.ds(0, channels, 2), :] = lagged(cells[0], cells[1]) * scale
        out_ref[b, pl.ds(1, channels, 2), :] = lagged(cells[2], cells[3]) * scale


def on_device(raw_strain, fir_taps, good_mask):
    segs, channels, samples = raw_strain.shape
    fibers, shares = lax.axis_size("fiber"), lax.axis_size("seg")
    rows = 2 * NF
    per = rows // shares
    size = channels // EDGE
    chunks = segs // size
    block = jax.ShapeDtypeStruct((shares, chunks, per + 1, size, channels), jnp.bfloat16)
    vmem = pl.BlockSpec(memory_space=pltpu.VMEM)
    hbm = pl.BlockSpec(memory_space=pltpu.HBM)
    edges = pltpu.VMEM((chunks, rows, size * EDGE), jnp.bfloat16)
    basis, smooth = dft_rows(samples, shares), smooth_rows(shares)
    dma = pltpu.SemaphoreType.DMA
    own, later = pl.pallas_call(
        functools.partial(spectra_kernel, fibers, shares),
        out_shape=(block, block),
        in_specs=[pl.BlockSpec(memory_space=pltpu.SMEM), hbm, hbm, hbm, hbm],
        out_specs=(vmem, vmem),
        scratch_shapes=[
            pltpu.VMEM((segs // 2, 2, channels, samples), jnp.bfloat16),
            pltpu.VMEM((chunks, 2, size, EDGE, samples), jnp.bfloat16),
            pltpu.VMEM(basis.shape, jnp.bfloat16),
            pltpu.VMEM(smooth.shape, jnp.bfloat16),
            pltpu.VMEM((segs, channels), jnp.int32),
            pltpu.VMEM((segs // 2, rows, 2 * channels), jnp.float32),
            edges, edges, edges, edges,
            pltpu.VMEM((2 * channels, 2 * channels), jnp.bfloat16),
            pltpu.VMEM((segs, channels), jnp.float32),
            pltpu.VMEM((rows * size, channels), jnp.float32),
            pltpu.VMEM(block.shape, jnp.bfloat16),
            dma((segs // 2,)),
            dma((2 * chunks,)),
            dma((3,)),
            dma((2, chunks)),
            dma((2, chunks)),
            dma((chunks, shares)),
            dma((chunks, shares)),
            dma((chunks, shares)),
            dma((chunks, shares)),
            dma((chunks,)),
        ],
        compiler_params=pltpu.CompilerParams(
            collective_id=0, has_side_effects=True, vmem_limit_bytes=VMEM_LIMIT
        ),
        name="spectra",
    )(
        fir_taps,
        *(
            pltpu.with_memory_space_constraint(x, pltpu.HBM)
            for x in (raw_strain, good_mask, jnp.asarray(basis), jnp.asarray(smooth))
        ),
    )

    bins = NF // shares
    step_bins = next(n for n in (12, 9, 6, 4, 3, 2, 1) if bins % n == 0)
    out = pl.pallas_call(
        functools.partial(cross_kernel, step_bins),
        grid=(bins // step_bins,),
        out_shape=jax.ShapeDtypeStruct((bins, 2 * channels, LAGS), jnp.float32),
        in_specs=[vmem, vmem],
        out_specs=pl.BlockSpec((step_bins, 2 * channels, LAGS), lambda i: (i, 0, 0)),
        scratch_shapes=[pltpu.VMEM((channels, LAGS), jnp.float32)],
        compiler_params=pltpu.CompilerParams(vmem_limit_bytes=40 * 2**20),
        name="cross",
    )(own, later)
    return out.reshape(bins, channels, 2, LAGS)


def solution(mesh):
    return jax.shard_map(
        on_device,
        mesh=mesh,
        in_specs=(P("seg", "fiber", None), P(), P("seg", "fiber")),
        out_specs=P("seg", "fiber", None, None),
        check_vma=False,
    )
```

```python
import functools
import math

import jax
import jax.numpy as jnp
import numpy as np
from jax import lax
from jax.experimental import pallas as pl
from jax.experimental.pallas import tpu as pltpu
from jax.sharding import PartitionSpec as P

NF = 144
LOW = 16
SMOOTH = 4
LAGS = 128
EDGE = 16

epsilon = 1e-06
water_share = 0.1
MESH = pl.DeviceIdType.MESH
VMEM_LIMIT = 40 * 2**20


def row_bins(shares):
    per = NF // shares
    return np.concatenate([np.tile(np.arange(k * per, (k + 1) * per), 2) for k in range(shares)])


def row_parts(shares):
    per = NF // shares
    return np.tile(np.repeat(np.arange(2), per), shares)


def dft_rows(samples, shares):
    bins, parts = row_bins(shares), row_parts(shares)
    index = ((bins[:, None] + LOW) * np.arange(samples)[None, :]) % samples
    angles = index.astype(np.float64) * (2.0 * math.pi / samples)
    return np.where(parts[:, None] == 0, np.cos(angles), -np.sin(angles)).astype(jnp.bfloat16)


def smooth_rows(shares):
    bins = row_bins(shares)
    return (np.abs(bins[:, None] - bins[None, :]) <= SMOOTH).astype(jnp.bfloat16)


def two_terms(x):
    hi = x.astype(jnp.bfloat16)
    return hi, (x - hi.astype(jnp.float32)).astype(jnp.bfloat16)


def mm(a, b):
    return jnp.dot(a, b, preferred_element_type=jnp.float32)


def mm_t(a, b):
    return lax.dot_general(a, b, (((1,), (1,)), ((), ())), preferred_element_type=jnp.float32)


def turned(x, shift):
    return pltpu.roll(x, shift, 1) if shift else x


def partner(seg, m):
    bit = 1
    while bit <= m:
        if m & bit:
            seg = seg + bit - 2 * bit * (seg // bit % 2)
        bit *= 2
    return seg


def taken(ref, q):
    shares, chunks, _, size, channels = ref.shape
    return ref[:, :, q].reshape(shares * chunks * size, channels)


def spectra_kernel(
    fibers, shares, taps_hbm, raw_ref, mask_ref, basis_hbm, smooth_hbm,
    own_ref, next_ref, part_ref, turn_ref,
    taps_ref, raw_v, edge_v, basis_ref, smooth_ref, flag_v, spec_v, out_l, out_r, in_l, in_r, band_v, mask_v,
    white_v, send_v,
    raw_sem, edge_sem, misc_sem, halo_send, halo_recv, own_send, own_recv, next_send, next_recv, local_sem,
):
    fib = lax.axis_index("fiber")
    seg = lax.axis_index("seg")
    segs, channels, _ = raw_ref.shape
    rows = basis_ref.shape[0]
    per = rows // shares
    taps = taps_ref.shape[0]
    half = (taps - 1) // 2
    has_prev = fib > 0
    has_next = fib < fibers - 1
    prev = jnp.maximum(fib - 1, 0)
    following = jnp.minimum(fib + 1, fibers - 1)
    size = channels // EDGE
    chunks = segs // size
    pairs = segs // 2
    chunk_pairs = size // 2

    taps_copy = pltpu.make_async_copy(taps_hbm, taps_ref, misc_sem.at[3])
    taps_copy.start()
    basis_copy = pltpu.make_async_copy(basis_hbm, basis_ref, misc_sem.at[0])
    basis_copy.start()
    edge_copies = [
        [
            pltpu.make_async_copy(
                raw_ref.at[pl.ds(c * size, size), pl.ds(start, EDGE), :],
                edge_v.at[c, i], edge_sem.at[2 * c + i],
            )
            for i, start in enumerate((0, channels - EDGE))
        ]
        for c in range(chunks)
    ]
    for copy in edge_copies[0]:
        copy.start()
    mask_copy = pltpu.make_async_copy(mask_ref, flag_v, misc_sem.at[2])
    mask_copy.start()
    raw_copies = [
        pltpu.make_async_copy(raw_ref.at[pl.ds(2 * p, 2)], raw_v.at[p], raw_sem.at[p])
        for p in range(pairs)
    ]
    for p, copy in enumerate(raw_copies):
        copy.start()
        if (p + 1) % chunk_pairs == 0 and (p + 1) // chunk_pairs < chunks:
            for edge in edge_copies[(p + 1) // chunk_pairs]:
                edge.start()
    smooth_copy = pltpu.make_async_copy(smooth_hbm, smooth_ref, misc_sem.at[1])
    smooth_copy.start()

    barrier = pltpu.get_barrier_semaphore()
    for m in range(1, shares):
        pl.semaphore_signal(
            barrier, inc=1, device_id=(fib, partner(seg, m)), device_id_type=MESH
        )
    @pl.when(has_prev)
    def _():
        pl.semaphore_signal(barrier, inc=1, device_id=(fib - 1, seg), device_id_type=MESH)
    @pl.when(has_next)
    def _():
        pl.semaphore_signal(barrier, inc=1, device_id=(fib + 1, seg), device_id_type=MESH)

    row = lax.broadcasted_iota(jnp.int32, (2 * channels, channels), 0)
    col = lax.broadcasted_iota(jnp.int32, (2 * channels, channels), 1)
    left = row - channels - EDGE
    right = row - EDGE
    place = jnp.where(row < channels, row, jnp.where(left < 0, left, right))
    place = jnp.where(row < channels + 2 * EDGE, place, 8 * channels)
    tap = place - col + half
    band = jnp.zeros((2 * channels, channels), jnp.float32)
    taps_copy.wait()
    for j in range(taps):
        band = jnp.where(tap == j, taps_ref[j], band)
    band_hi, band_lo = two_terms(band)
    band_v[:, :channels] = band_hi
    band_v[:, channels:] = band_lo

    @pl.when(jnp.logical_not(has_prev))
    def _():
        in_l[...] = jnp.zeros_like(in_l)
    @pl.when(jnp.logical_not(has_next))
    def _():
        in_r[...] = jnp.zeros_like(in_r)
        next_ref[...] = jnp.zeros_like(next_ref)

    def transform_edges(c):
        for copy in edge_copies[c]:
            copy.wait()
        ends = mm_t(basis_ref[...], edge_v[c].reshape(2 * channels, -1)).astype(jnp.bfloat16)
        out_l[c] = ends[:, :channels]
        out_r[c] = ends[:, channels:]

    basis_copy.wait()
    transform_edges(0)
    sides = (fib + fibers - 1) // fibers + (2 * fibers - 2 - fib) // fibers
    pl.semaphore_wait(barrier, shares - 1 + sides)

    to_prev = [
        pltpu.make_async_remote_copy(
            src_ref=out_l.at[c], dst_ref=in_r.at[c],
            send_sem=halo_send.at[0, c], recv_sem=halo_recv.at[0, c],
            device_id=(prev, seg), device_id_type=MESH,
        )
        for c in range(chunks)
    ]
    to_next = [
        pltpu.make_async_remote_copy(
            src_ref=out_r.at[c], dst_ref=in_l.at[c],
            send_sem=halo_send.at[1, c], recv_sem=halo_recv.at[1, c],
            device_id=(following, seg), device_id_type=MESH,
        )
        for c in range(chunks)
    ]
    def send_edges(c):
        @pl.when(has_prev)
        def _():
            to_prev[c].start()
        @pl.when(has_next)
        def _():
            to_next[c].start()

    send_edges(0)
    mask_copy.wait()
    mask_v[...] = flag_v[...].astype(jnp.float32)
    for c in range(chunks):
        flags = mask_v[c * size : (c + 1) * size, :].astype(jnp.bfloat16)
        for k in range(shares):
            send_v[k, c, per] = flags

    lane = lax.broadcasted_iota(jnp.int32, (rows, channels), 1)

    def transform(c):
        for p in range(c * chunk_pairs, (c + 1) * chunk_pairs):
            raw_copies[p].wait()
            spec_v[p] = mm_t(basis_ref[...], raw_v[p].reshape(2 * channels, -1))

    def whiten(c):
        def whiten_pair(i, carry):
            p = c * chunk_pairs + i
            lefts = in_l[c].astype(jnp.float32)
            rights = in_r[c].astype(jnp.float32)
            parts = []
            for h in range(2):
                slot = 2 * i + h
                l_roll = (channels - slot * EDGE) % channels
                r_roll = (channels + EDGE - slot * EDGE) % channels
                edges = jnp.where(lane < EDGE, turned(lefts, l_roll), turned(rights, r_roll))
                hi, lo = two_terms(spec_v[p, :, h * channels : (h + 1) * channels])
                wide = mm(jnp.concatenate([hi, edges.astype(jnp.bfloat16)], axis=1), band_v[...])
                parts.append(
                    wide[:, :channels] + wide[:, channels:] + mm(lo, band_v[:channels, :channels])
                )
            filtered = jnp.concatenate(parts, axis=1)
            power = filtered * filtered
            smooth = mm(smooth_ref[...], power.astype(jnp.bfloat16))
            total = jnp.sum(power, axis=0, keepdims=True)
            level = smooth * (1.0 / (2 * SMOOTH + 1)) + (total * (water_share / NF) + epsilon)
            good = jnp.concatenate(
                [mask_v[pl.ds(2 * p, 1), :], mask_v[pl.ds(2 * p + 1, 1), :]], axis=1
            )
            white = filtered * (lax.rsqrt(level) * good)
            white_v[pl.ds(2 * i, rows, size), :] = white[:, :channels]
            white_v[pl.ds(2 * i + 1, rows, size), :] = white[:, channels:]
            return carry

        for i in range(chunk_pairs):
            whiten_pair(i, 0)
        for k in range(shares):
            send_v[k, c, :per] = (
                white_v[k * per * size : (k + 1) * per * size, :]
                .reshape(per, size, channels)
                .astype(jnp.bfloat16)
            )

    def to_own(c, m):
        other = partner(seg, m)
        return pltpu.make_async_remote_copy(
            src_ref=send_v.at[other, c], dst_ref=own_ref.at[seg, c],
            send_sem=own_send.at[c, m], recv_sem=own_recv.at[c, m],
            device_id=(fib, other), device_id_type=MESH,
        )

    def from_own(c, m):
        other = partner(seg, m)
        return pltpu.make_async_remote_copy(
            src_ref=send_v.at[other, c], dst_ref=own_ref.at[other, c],
            send_sem=own_send.at[c, m], recv_sem=own_recv.at[c, m],
            device_id=(fib, other), device_id_type=MESH,
        )

    def hand_on(c, m):
        source = partner(seg, m)
        block = send_v if m == 0 else own_ref
        return pltpu.make_async_remote_copy(
            src_ref=block.at[source, c], dst_ref=next_ref.at[source, c],
            send_sem=next_send.at[c, m], recv_sem=next_recv.at[c, m],
            device_id=(prev, seg), device_id_type=MESH,
        )

    def kept(c):
        return pltpu.make_async_copy(send_v.at[seg, c], own_ref.at[seg, c], local_sem.at[c])

    def give(c):
        @pl.when(has_prev)
        def _():
            hand_on(c, 0).start()
        for m in range(1, shares):
            to_own(c, m).start()
        kept(c).start()

    def relay(c, m):
        from_own(c, m).wait_recv()
        @pl.when(has_prev)
        def _():
            hand_on(c, m).start()

    smooth_copy.wait()
    waiting = []
    for c in range(chunks):
        transform(c)
        if c + 1 < chunks:
            transform_edges(c + 1)
            send_edges(c + 1)
        if waiting:
            relay(*waiting.pop(0))
        @pl.when(has_prev)
        def _():
            to_next[c].wait_recv()
        @pl.when(has_next)
        def _():
            to_prev[c].wait_recv()
        whiten(c)
        give(c)
        waiting += [(c, m) for m in range(1, shares)]
    for item in waiting:
        relay(*item)
    for c in range(chunks):
        kept(c).wait()

    bins = per // 2
    group = next(n for n in (6, 4, 3, 2, 1) if bins % n == 0)

    def own_products(i, carry):
        for b in range(group):
            f = i * group + b
            re, im = taken(own_ref, f), taken(own_ref, bins + f)
            turned_left = jnp.concatenate([re, im], axis=0).T
            right = jnp.concatenate(
                [jnp.concatenate([re, im], axis=1), jnp.concatenate([im, -re], axis=1)], axis=0
            )
            turn_ref[f] = turned_left
            part_ref[f] = mm(turned_left, right)
        return carry

    lax.fori_loop(0, bins // group, own_products, 0)
    for c in range(chunks):
        for m in range(1, shares):
            to_own(c, m).wait_send()
    @pl.when(has_prev)
    def _():
        for c in range(chunks):
            to_prev[c].wait_send()
            for m in range(shares):
                hand_on(c, m).wait_send()
    @pl.when(has_next)
    def _():
        for c in range(chunks):
            to_next[c].wait_send()
            for m in range(shares):
                hand_on(c, m).wait_recv()


def cross_kernel(step_bins, own_ref, next_ref, part_ref, turn_ref, out_ref, scale_v):
    i = pl.program_id(0)
    shares, chunks, rows, size, channels = own_ref.shape
    bins = (rows - 1) // 2
    row = lax.broadcasted_iota(jnp.int32, (channels, channels), 0)
    col = lax.broadcasted_iota(jnp.int32, (channels, channels), 1)

    lags = (col + row + 1) % channels

    def lagged(near, far):
        chosen = jnp.where(col > row, near, far)
        return jnp.take_along_axis(chosen, lags, axis=1)

    def grams(a, b):
        return lax.dot_general(a, b, (((0,), (0,)), ((), ())), preferred_element_type=jnp.float32)

    @pl.when(i == 0)
    def _():
        here = taken(own_ref, rows - 1)
        counts = lagged(grams(here, here), grams(here, taken(next_ref, rows - 1)))
        scale_v[...] = 1.0 / jnp.maximum(counts, 1.0)

    scale = scale_v[...]
    for b in range(step_bins):
        f = i * step_bins + b
        re, im = taken(next_ref, f), taken(next_ref, bins + f)
        right = jnp.concatenate(
            [jnp.concatenate([re, im], axis=1), jnp.concatenate([im, -re], axis=1)], axis=0
        )
        far = mm(turn_ref[f], right)
        for n in range(2):
            cells = slice(n * channels, (n + 1) * channels)
            out_ref[b, pl.ds(n, channels, 2), :] = lagged(part_ref[f, :, cells], far[:, cells]) * scale


def on_device(raw_strain, fir_taps, good_mask):
    segs, channels, samples = raw_strain.shape
    fibers, shares = lax.axis_size("fiber"), lax.axis_size("seg")
    rows = 2 * NF
    per = rows // shares
    size = channels // EDGE
    chunks = segs // size
    block = jax.ShapeDtypeStruct((shares, chunks, per + 1, size, channels), jnp.bfloat16)
    vmem = pl.BlockSpec(memory_space=pltpu.VMEM)
    hbm = pl.BlockSpec(memory_space=pltpu.HBM)
    edges = pltpu.VMEM((chunks, rows, size * EDGE), jnp.bfloat16)
    basis, smooth = dft_rows(samples, shares), smooth_rows(shares)
    dma = pltpu.SemaphoreType.DMA
    spectral = pl.pallas_call(
        functools.partial(spectra_kernel, fibers, shares),
        out_shape=(
            block,
            block,
            jax.ShapeDtypeStruct((per // 2, channels, 2 * channels), jnp.float32),
            jax.ShapeDtypeStruct((per // 2, channels, 2 * shares * segs), jnp.bfloat16),
        ),
        in_specs=[hbm] * 5,
        out_specs=(vmem,) * 4,
        scratch_shapes=[
            pltpu.SMEM(fir_taps.shape, jnp.float32),
            pltpu.VMEM((segs // 2, 2, channels, samples), jnp.bfloat16),
            pltpu.VMEM((chunks, 2, size, EDGE, samples), jnp.bfloat16),
            pltpu.VMEM(basis.shape, jnp.bfloat16),
            pltpu.VMEM(smooth.shape, jnp.bfloat16),
            pltpu.VMEM((segs, channels), jnp.int32),
            pltpu.VMEM((segs // 2, rows, 2 * channels), jnp.float32),
            edges, edges, edges, edges,
            pltpu.VMEM((2 * channels, 2 * channels), jnp.bfloat16),
            pltpu.VMEM((segs, channels), jnp.float32),
            pltpu.VMEM((rows * size, channels), jnp.float32),
            pltpu.VMEM(block.shape, jnp.bfloat16),
            dma((segs // 2,)),
            dma((2 * chunks,)),
            dma((4,)),
            dma((2, chunks)),
            dma((2, chunks)),
            dma((chunks, shares)),
            dma((chunks, shares)),
            dma((chunks, shares)),
            dma((chunks, shares)),
            dma((chunks,)),
        ],
        compiler_params=pltpu.CompilerParams(
            collective_id=0, has_side_effects=True, vmem_limit_bytes=VMEM_LIMIT
        ),
        name="spectra",
    )(
        *(
            pltpu.with_memory_space_constraint(x, pltpu.HBM)
            for x in (fir_taps, raw_strain, good_mask, jnp.asarray(basis), jnp.asarray(smooth))
        ),
    )

    bins = NF // shares
    step_bins = next(n for n in (12, 9, 6, 4, 3, 2, 1) if bins % n == 0)
    out = pl.pallas_call(
        functools.partial(cross_kernel, step_bins),
        grid=(bins // step_bins,),
        out_shape=jax.ShapeDtypeStruct((bins, 2 * channels, LAGS), jnp.float32),
        in_specs=[vmem] * 4,
        out_specs=pl.BlockSpec((step_bins, 2 * channels, LAGS), lambda i: (i, 0, 0)),
        scratch_shapes=[pltpu.VMEM((channels, LAGS), jnp.float32)],
        compiler_params=pltpu.CompilerParams(vmem_limit_bytes=VMEM_LIMIT),
        name="cross",
    )(*spectral)
    return out.reshape(bins, channels, 2, LAGS)


def solution(mesh):
    return jax.shard_map(
        on_device,
        mesh=mesh,
        in_specs=(P("seg", "fiber", None), P(), P("seg", "fiber")),
        out_specs=P("seg", "fiber", None, None),
        check_vma=False,
    )
```
